256 devices in a mesh: seq: 32 (over z, x_hi, core), dp: 8 (over x_lo, y).
Axes of the slice: x: 4 (x_hi: 2, x_lo: 2; x = x_hi * 2 + x_lo), y: 4, z: 8, core: 2. Of those that a mesh axis runs over, the one named last changes fastest.
Arguments:
- activations: bfloat16 [8, 4096, 768], P('dp', 'seq'), may hold values from -6 to 6
- cotangent: bfloat16 [8, 4096, 768], P('dp', 'seq'), may hold values from -6 to 6
- weights: bfloat16 [3840, 768], P(('seq', 'dp')), may hold values from -0.09375 to 0.09375
- norm_gain: float32 [768], replicated, may hold values from 0.25 to 1.75
- pairing: int32 [768], replicated, may hold values from 0 to 767, as said below
Outputs:
- combined: bfloat16 [8, 4096, 768], P('dp', 'seq')
- grad_input: bfloat16 [8, 4096, 768], P('dp', 'seq')
- grad_kernel: float32 [3840, 768], P(('seq', 'dp'))
- grad_gain: float32 [768], P(('seq', 'dp'))
The draws below stay inside these ranges and needn't reach their ends.
Inputs may be any that keep to these rules, and one draw needn't show every extreme that they name: pairing is an involution without fixed points: pairing[pairing[c]] = c != pairing[c].
All inputs are finite; a program needn't handle non-finite values.
Results may differ from the reference program's by a relative error of at most 0.0055.
Values may be sent and summed in bfloat16 or wider, within the bound.
A program may use at most 192 MiB of HBM per device.

```python
import jax
import jax.numpy as jnp
from jax import lax

CHANNELS = 768
TAPS = 5
LENGTH = 4096
SEQS = 8


def draw_pairing(key, part):
    shuffled = jax.random.permutation(jax.random.fold_in(key, 7), CHANNELS).astype(jnp.int32)
    lead_half = shuffled[0::2]
    tail_half = shuffled[1::2]
    result = jnp.zeros((CHANNELS,), jnp.int32)
    result = result.at[lead_half].set(tail_half).at[tail_half].set(lead_half)
    return result.astype(jnp.int32)


def strengthened(entries, own_key, source, target, shards_of, factor):
    owner, partner = [(jnp.arange(entries.shape[position]) // (entries.shape[position] // shards_of)).reshape([-1 if axis == position else 1 for axis in range(entries.ndim)]) for position in (source, target)]
    chosen = jax.random.permutation(own_key, shards_of)[partner]
    strong = (owner == chosen) | (owner == (partner + shards_of // 2) % shards_of)
    return jnp.where(strong, factor * entries, entries)


def block_levels(own_key, shape, shards, least, top_value):
    level = 1.0
    for dim, shards_of in shards:
        steps = jax.random.uniform(jax.random.fold_in(jax.random.fold_in(own_key, 6), dim), (shards_of,), jnp.float32, least / len(shards), top_value / len(shards))
        level = level * jnp.repeat(jnp.exp(steps), shape[dim] // shards_of).reshape((-1,) + (1,) * (len(shape) - 1 - dim))
    return level


def scatter_about(rng, dims, scale, bound, shards=(), kind=jnp.bfloat16):
    values = scale * jax.random.normal(rng, dims, jnp.float32)
    if shards:
        values = values * block_levels(rng, dims, shards, -0.22, 0.18)
    return jnp.clip(values, -bound, bound).astype(kind)


def heavy_noise(own_key, dims, scale, reach, shards, heavy, kind=jnp.bfloat16):
    values = scale * jax.random.normal(own_key, dims, jnp.float32)
    if shards:
        values = values * block_levels(own_key, dims, shards, -0.22, 0.18)
    return jnp.clip(strengthened(values, jax.random.fold_in(own_key, 3), *heavy), -reach, reach).astype(kind)


def setup_inputs(seed: int = 0) -> dict:
    key_of = jax.random.split(jax.random.key(seed), 6)
    activations = heavy_noise(key_of[0], (SEQS, LENGTH, CHANNELS), 1.0, 6.0, ((0, 8), (1, 32)), (1, 2, 32, 2.75))
    cotangent = scatter_about(key_of[1], (SEQS, LENGTH, CHANNELS), 1.0, 6.0, ((0, 8), (1, 32)))
    weights = scatter_about(key_of[2], (TAPS * CHANNELS, CHANNELS), (TAPS * CHANNELS) ** -0.5, 0.09375, ((0, 256),))
    norm_gain = jnp.clip(1.0 + 0.15 * jax.random.normal(key_of[3], (CHANNELS,), jnp.float32), 0.25, 1.75)
    pairing = draw_pairing(jax.random.fold_in(key_of[5], 71), 0)
    return {"activations": activations, "cotangent": cotangent, "weights": weights, "norm_gain": norm_gain, "pairing": pairing}


epsilon = 1e-06

def strand(values_in, cot_half, kernel, norm_gain):
    values = values_in.astype(jnp.float32)
    inverse_rms = lax.rsqrt(lax.optimization_barrier(jnp.mean(values * values, -1, keepdims=True)) + epsilon)
    normed = (values * inverse_rms * norm_gain).astype(jnp.bfloat16)
    padded = jnp.pad(normed, ((2, 2), (0, 0)))
    windows = jnp.concatenate([padded[offset:offset + LENGTH] for offset in range(TAPS)], -1)
    preact = jnp.dot(windows, kernel, preferred_element_type=jnp.float32)
    result = values + jax.nn.gelu(preact)
    _, pullback = jax.vjp(jax.nn.gelu, preact)
    grad_pre = pullback(cot_half)[0].astype(jnp.bfloat16)
    kernel_term = jnp.dot(windows.T, grad_pre, preferred_element_type=jnp.float32)
    grad_pad = jnp.pad(grad_pre, ((2, 2), (0, 0)))
    back_windows = jnp.concatenate([grad_pad[TAPS - 1 - offset:TAPS - 1 - offset + LENGTH] for offset in range(TAPS)], -1)
    kernel_t = kernel.reshape(TAPS, CHANNELS, CHANNELS).transpose(0, 2, 1).reshape(TAPS * CHANNELS, CHANNELS)
    grad_normed = jnp.dot(back_windows, kernel_t, preferred_element_type=jnp.float32)
    gain_term = lax.optimization_barrier(jnp.sum(grad_normed * values * inverse_rms, 0))
    scaled = grad_normed * norm_gain
    grad_values = cot_half + inverse_rms * scaled - values * inverse_rms ** 3 * lax.optimization_barrier(jnp.mean(scaled * values, -1, keepdims=True))
    return (result, grad_values, kernel_term, gain_term)

def reference(activations, cotangent, weights, norm_gain, pairing):

    def one_sequence(pieces):
        seq_in, seq_cot = pieces
        half_cot = 0.5 * seq_cot.astype(jnp.float32)
        fwd_out, fwd_grad, fwd_kernel, fwd_gain = strand(seq_in, half_cot, weights, norm_gain)
        rev_in = seq_in[::-1][:, pairing]
        rev_cot = half_cot[::-1][:, pairing]
        rev_out, rev_grad, rev_kernel, rev_gain = strand(rev_in, rev_cot, weights, norm_gain)
        out_round = lax.optimization_barrier(rev_out.astype(jnp.bfloat16))[::-1][:, pairing]
        grad_round = lax.optimization_barrier(rev_grad.astype(jnp.bfloat16))[::-1][:, pairing]
        combined = (0.5 * (fwd_out + out_round.astype(jnp.float32))).astype(jnp.bfloat16)
        grad_input = (fwd_grad + grad_round.astype(jnp.float32)).astype(jnp.bfloat16)
        return (combined, grad_input, fwd_kernel + rev_kernel, fwd_gain + rev_gain)
    combined, grad_input, kernels, gains = lax.map(one_sequence, (activations, cotangent))
    return (combined, grad_input, lax.optimization_barrier(jnp.sum(kernels, 0)), lax.optimization_barrier(jnp.sum(gains, 0)))
```

```python
import functools

import jax
import jax.numpy as jnp
from jax import lax
from jax.experimental import pallas as pl
from jax.experimental.pallas import tpu as pltpu
from jax.sharding import PartitionSpec as P

EPS = 1e-06
MESH = pl.DeviceIdType.MESH
BF = jnp.bfloat16
F32 = jnp.float32

C = 768
HALF = 384
OWN = 128
TAPS = 5
ROWS = 288
CHIP0 = 16
NZ, NX, NY = 8, 4, 4
MSGS = 128


def rem(a, n):
    return lax.rem(a, jnp.int32(n))


def div(a, n):
    return lax.div(a, jnp.int32(n))


def place(z, x, y, c):
    return (z * 4 + div(x, 2) * 2 + c, rem(x, 2) * 4 + y)


def loop(count, body):
    def step(i, carry):
        body(i)
        return carry

    lax.fori_loop(0, count, step, 0)


def dot(a, b):
    return jnp.dot(a, b, preferred_element_type=F32)


def dot_nt(a, b):
    return lax.dot_general(a, b, (((1,), (1,)), ((), ())), preferred_element_type=F32)


def gelu_parts(x):
    k = 0.7978845608028654
    x2 = x * x
    t = jnp.tanh(k * (x + 0.044715 * x2 * x))
    cdf = 0.5 * (1.0 + t)
    slope = cdf + x * (0.5 * (1.0 - t * t)) * (k * (1.0 + 3 * 0.044715 * x2))
    return x * cdf, slope


def kernel(
    act, cot, wsh, gain, pairing,
    out_ref, grad_ref, gk_ref, gg_ref,
    xe, ce, xp, cp, perm, perm_half, inv_ref, nf, wnd, wp, wpt, wb, dwb, acc,
    resf, resr, gpf, gpb, wun, gnb, gnx, rfx, rrx,
    slot4, slot8, red4, red8, slot_y, slot_x, slot_2x, one01, one2, slot_z, slot_2y,
    gsum, gz, gx, gy, gp_, fin, finx,
    send, recv, local, halo,
):
    s = lax.axis_index("seq")
    d = lax.axis_index("dp")
    z, xh, core = div(s, 4), rem(div(s, 2), 2), rem(s, 2)
    xl, y = div(d, 4), rem(d, 4)
    x = xh * 2 + xl
    m = z * 2 + xh
    other = 1 - core

    def in_x(o):
        return place(z, rem(x + o, NX), y, core)

    def in_y(o):
        return place(z, x, rem(y + o, NY), core)

    def in_z(o):
        return place(rem(z + o, NZ), x, y, core)

    partner = place(z, x, y, other)

    def chip_m(mm, c):
        return place(div(mm, 2), rem(mm, 2) * 2 + xl, y, c)

    barrier = pltpu.get_barrier_semaphore()
    met = [partner]
    met += [in_x(o) for o in range(1, NX)] + [in_y(o) for o in range(1, NY)]
    met += [in_z(o) for o in range(1, NZ)]
    met += [chip_m(rem(m + o, 16), c) for o in (1, 15) for c in (0, 1)]
    for who in met:
        pl.semaphore_signal(barrier, inc=1, device_id=who, device_id_type=MESH)
    pl.semaphore_wait(barrier, len(met))

    started = []

    def put(src, dst, who):
        i = len(started)
        copy = pltpu.make_async_remote_copy(
            src_ref=src, dst_ref=dst, send_sem=send.at[i], recv_sem=recv.at[i],
            device_id=who, device_id_type=MESH,
        )
        copy.start()
        started.append(copy)
        return copy

    def keep(src, dst, i):
        copy = pltpu.make_async_copy(src, dst, local.at[i])
        copy.start()
        return copy

    mine16 = pl.ds(pl.multiple_of(core * 16, 16), 16)
    mine = pl.ds(pl.multiple_of(CHIP0 + core * OWN, 16), OWN)
    theirs = pl.ds(pl.multiple_of(CHIP0 + other * OWN, 16), OWN)
    w_there = put(wsh.at[other], wb.at[:, z, x, y, mine16, :], partner)
    w_here = keep(wsh.at[core], wb.at[:, z, x, y, mine16, :], 0)
    x_here = keep(act.at[0], xe.at[mine], 1)
    c_here = keep(cot.at[0], ce.at[mine], 2)
    x_there = put(act.at[0], xe.at[mine], partner)
    edge_src = pl.ds(pl.multiple_of(core * 112, 16), 16)
    edge_dst = pl.ds(pl.multiple_of(other * 272, 16), 16)
    toward = rem(m + core * 2 + 15, 16)
    edges = []
    for c in (0, 1):
        for k, (src, dst) in enumerate(((act, xe), (cot, ce))):
            i = len(edges)
            copy = pltpu.make_async_remote_copy(
                src_ref=src.at[0, edge_src], dst_ref=dst.at[edge_dst],
                send_sem=halo.at[2 + i, 0], recv_sem=halo.at[k, core],
                device_id=chip_m(toward, c), device_id_type=MESH,
            )
            copy.start()
            edges.append(copy)
    c_there = put(cot.at[0], ce.at[mine], partner)

    w_here.wait()
    w_there.wait_recv()
    first01 = [
        put(wb.at[pl.ds(0, 2), z, x, y], wb.at[pl.ds(0, 2), z, x, y], in_z(o)) for o in range(1, NZ)
    ]
    first2 = [put(wb.at[2, z, x, y], wb.at[2, z, x, y], in_y(o)) for o in range(1, NY)]

    perm[...] = (lax.broadcasted_iota(jnp.int32, (C, C), 0) == pairing[...]).astype(F32).astype(BF)
    half_cols = pl.ds(pl.multiple_of(core * HALF, 128), HALF)
    other_cols = pl.ds(pl.multiple_of(other * HALF, 128), HALF)
    perm_half[...] = (
        (lax.broadcasted_iota(jnp.int32, (C, HALF), 0) == pairing[:, half_cols])
        .astype(F32).astype(BF)
    )

    x_here.wait()
    c_here.wait()
    x_there.wait_recv()
    c_there.wait_recv()
    for k, dst in enumerate((xe, ce)):
        for side in (0, 1):
            into = dst.at[pl.ds(272 * (1 - side), 16)]
            pltpu.make_async_remote_copy(
                src_ref=into, dst_ref=into, send_sem=halo.at[2, 0], recv_sem=halo.at[k, side],
                device_id=partner, device_id_type=MESH,
            ).wait_recv()

    def inside(first, count, width):
        row = lax.broadcasted_iota(jnp.int32, (count, width), 0) + first
        low = jnp.where(m > 0, 0, CHIP0)
        high = jnp.where(m < 15, ROWS, ROWS - 16)
        return (row >= low) & (row < high)

    def norm_rows(i):
        at = pl.ds(pl.multiple_of(i * 32, 32), 32)
        raw = xe[at, :]
        values = jnp.where(inside(i * 32, 32, C), raw.astype(F32), 0.0)
        inverse = lax.rsqrt(jnp.mean(values * values, -1, keepdims=True) + EPS)
        inv_ref[at, :] = inverse
        swapped = dot(values.astype(BF), perm[...])
        xp[at, :] = swapped.astype(BF)
        into = pl.ds(pl.multiple_of(8 + i * 32, 8), 32)
        nf[0, into, :] = (values * inverse * gain[...]).astype(BF).astype(F32)
        nf[1, into, :] = (swapped * inverse * gain[...]).astype(BF).astype(F32)
        cp[at, :] = dot(ce[at, :], perm[...]).astype(BF)

    nf[:, 0:8, :] = jnp.zeros((2, 8, C), F32)
    nf[:, 8 + ROWS :, :] = jnp.zeros((2, 8, C), F32)
    wnd[:, TAPS * C :] = jnp.zeros((2 * ROWS, 128), BF)
    loop(ROWS // 32, norm_rows)

    for copy in first2:
        copy.wait_recv()
    second2 = [put(wb.at[2, z, x], wb.at[2, z, x], in_x(o)) for o in range(1, NX)]

    def window_cols(i):
        cols = pl.ds(pl.multiple_of(i * 128, 128), 128)
        for strand in (0, 1):
            for k in range(TAPS):
                shift = (k - 2) if strand == 0 else (2 - k)
                wnd[strand * ROWS : (strand + 1) * ROWS, pl.ds(pl.multiple_of(k * C + i * 128, 128), 128)] = nf[
                    strand, 8 + shift : 8 + shift + ROWS, cols
                ].astype(BF)

    loop(C // 128, window_cols)

    for copy in first01:
        copy.wait_recv()
    second0 = [put(wb.at[0, :, x, y], wb.at[0, :, x, y], in_y(o)) for o in range(1, NY)]
    second1 = [put(wb.at[1, :, x, y], wb.at[1, :, x, y], in_x(o)) for o in range(1, NX)]

    def source_of(slot, g):
        r = slot & 15
        c, yy, xx = (slot >> 4) & 1, (slot >> 5) & 3, slot >> 7
        src = ((c * 2 + xx) * 4 + yy) * 15 + r + 16 * rem(15 * g, 8)
        return jnp.where(r < 15, src, -1)

    def iota(shape, axis):
        return lax.broadcasted_iota(jnp.int32, shape, axis)

    def onehot(flag):
        return flag.astype(F32).astype(BF)

    def pad_group(g):
        cols = pl.ds(pl.multiple_of(div(15 * g, 8) * 128, 128), 384)
        spread = onehot(iota((384, 256), 0) == source_of(iota((384, 256), 1), g))
        into = pl.ds(pl.multiple_of(g * 256, 256), 256)
        wp[:, into] = dot(wnd[:, cols], spread).astype(BF)

    def pad_group_t(g):
        cols = pl.ds(pl.multiple_of(div(15 * g, 8) * 128, 128), 384)
        spread = onehot(iota((256, 384), 1) == source_of(iota((256, 384), 0), g))
        into = pl.ds(pl.multiple_of(g * 256, 256), 256)
        for strand in (0, 1):
            rows = slice(strand * ROWS + CHIP0, strand * ROWS + CHIP0 + 256)
            wpt[into, strand * 256 : (strand + 1) * 256] = dot_nt(spread, wnd[rows, cols]).astype(BF)

    loop(16, pad_group)

    def part(ref, colour, coord, half):
        if colour == 0:
            return ref.at[0, pl.ds(half * 4, 4), coord]
        if colour == 1:
            return ref.at[1, pl.ds(half * 4, 4), :, coord]
        return ref.at[2, coord, pl.ds(half * 2, 2)]

    rings = ((x, NX, in_x), (y, NY, in_y), (z, NZ, in_z))

    def limit(n, sign, half):
        return n // 2 if (half == 0) == (sign == 1) else n // 2 - 1

    def ring_send(colour, sign, half, hop):
        q, n, who = rings[colour]
        held = part(wb, colour, rem(q - sign * (hop - 1) + n, n), half)
        return put(held, held, who(1 if sign == 1 else n - 1))

    ways = ((1, 0), (-1, 1), (1, 1), (-1, 0))

    for copy in second2:
        copy.wait_recv()
    live = {}
    for sign, half in ways:
        live[2, sign, half] = ring_send(2, sign, half, 1)
    for copy in second0:
        copy.wait_recv()
    for sign, half in ways:
        live[0, sign, half] = ring_send(0, sign, half, 1)
    for copy in second1:
        copy.wait_recv()
    for sign, half in ways:
        live[1, sign, half] = ring_send(1, sign, half, 1)

    loop(16, pad_group_t)

    for hop in range(1, NZ // 2 + 1):
        for colour in (2, 0, 1):
            n = rings[colour][1]
            for sign, half in ways:
                if hop > limit(n, sign, half):
                    continue
                live[colour, sign, half].wait_recv()
                if hop < limit(n, sign, half):
                    live[colour, sign, half] = ring_send(colour, sign, half, hop + 1)

    def weights(i, groups):
        pieces = []
        for colour in range(3):
            got = wb[colour].reshape(16, 2 * NY * 64, 128) if groups is None else None
            pieces.append(got)
        return pieces

    def group_of(ref, zz, first):
        return jnp.concatenate(
            [ref[j, zz, pl.ds(first, 2)].reshape(256, 128) for j in range(3)], axis=1
        )

    def forward_rows(zz):
        right = jnp.concatenate(
            [wb[j, zz].reshape(512, 128) for j in range(3)], axis=1
        )
        return dot(wp[:, pl.ds(pl.multiple_of(zz * 512, 512), 512)], right)

    acc[...] = jnp.zeros((2 * ROWS, HALF), F32)

    def forward_step(zz):
        acc[...] += forward_rows(zz)

    loop(NZ, forward_step)

    def gelu_rows(strand):
        def body(i):
            at = pl.ds(pl.multiple_of(i * 32, 32), 32)
            pre = acc[pl.ds(pl.multiple_of(strand * ROWS + i * 32, 32), 32), :]
            value, slope = gelu_parts(pre)
            if strand == 0:
                resf[at, :] = xe[at, half_cols].astype(F32) + value
                g = ce[at, half_cols].astype(F32)
            else:
                resr[at, :] = (xp[at, half_cols].astype(F32) + value).astype(BF)
                g = cp[at, half_cols].astype(F32)
            gp = jnp.where(inside(i * 32, 32, HALF), 0.5 * g * slope, 0.0).astype(BF)
            gpb[strand, at, :] = gp
            gpf[strand, pl.ds(pl.multiple_of(8 + i * 32, 8), 32), :] = gp.astype(F32)

        return body

    loop(ROWS // 32, gelu_rows(0))
    loop(ROWS // 32, gelu_rows(1))

    def dw_group(g):
        zz, hh = div(g, 2), rem(g, 2) * 2
        right = jnp.concatenate(
            [gpb[0, CHIP0 : CHIP0 + 256, :], gpb[1, CHIP0 : CHIP0 + 256, :]], axis=0
        )
        got = dot(wpt[pl.ds(pl.multiple_of(g * 256, 256), 256), :], right).astype(BF)
        for j in range(3):
            dwb[j, zz, pl.ds(hh, 2)] = got[:, j * 128 : (j + 1) * 128].reshape(2, NY, 32, 128)

    loop(16, dw_group)

    def ring_slot(colour, sign, half, dist):
        way = ways.index((sign, half))
        if colour == 2:
            return slot8.at[way, dist - 1]
        return slot4.at[colour, way, dist - 1]

    def ring_give(colour, sign, half, dist, src):
        q, n, who = rings[colour]
        return put(src, ring_slot(colour, sign, half, dist), who(1 if sign == 1 else n - 1))

    for colour in (2, 0, 1):
        q, n, who = rings[colour]
        for sign, half in ways:
            dist = limit(n, sign, half)
            src = part(dwb, colour, rem(q + sign * dist + n, n), half)
            live[colour, sign, half] = ring_give(colour, sign, half, dist, src)

    there = pl.ds(pl.multiple_of(CHIP0 + other * OWN, 16), OWN)
    f_there = put(resf.at[there], rfx, partner)
    r_there = put(resr.at[there], rrx, partner)

    def pack_group(g):
        zz, hh = div(g, 2), rem(g, 2) * 2
        gather = onehot(iota((240, 256), 0) == source_of(iota((240, 256), 1), 0))
        right = group_of(wb, zz, hh)
        wun[pl.ds(pl.multiple_of(g * 240, 16), 240), :] = dot(gather, right).astype(BF)

    def ring_step(colour, hop):
        q, n, who = rings[colour]
        for sign, half in ways:
            dist = limit(n, sign, half) - (hop - 1)
            if dist < 1:
                continue
            live[colour, sign, half].wait_recv()
            if dist > 1:
                got = ring_slot(colour, sign, half, dist)
                add = part(dwb, colour, rem(q + sign * (dist - 1) + n, n), half)
                got[...] = (got[...].astype(F32) + add[...].astype(F32)).astype(BF)
                live[colour, sign, half] = ring_give(colour, sign, half, dist - 1, got)

    def ring_total(colour, half):
        q = rings[colour][0]
        total = part(dwb, colour, q, half)[...].astype(F32)
        for sign in (1, -1):
            total = total + ring_slot(colour, sign, half, 1)[...].astype(F32)
        return total.astype(BF)

    loop(16, pack_group)

    ring_step(2, 1)
    ring_step(0, 1)
    ring_step(1, 1)

    gpf[:, 0:8, :] = jnp.zeros((2, 8, HALF), F32)
    gpf[:, 8 + ROWS :, :] = jnp.zeros((2, 8, HALF), F32)

    def normed_grad(block):
        first = 8 + CHIP0 + block * OWN
        for strand in (0, 1):
            total = None
            for k in range(TAPS):
                shift = (2 - k) if strand == 0 else (k - 2)
                left = gpf[strand, first + shift : first + shift + OWN, :].astype(BF)
                term = dot_nt(left, wun[k * C : (k + 1) * C, :])
                total = term if total is None else total + term
            gnb[block, strand] = total

    normed_grad(0)
    ring_step(2, 2)
    ring_step(0, 2)
    ring_step(1, 2)
    red4[0, 0:4] = ring_total(0, 0)
    red4[0, 4:8] = ring_total(0, 1)
    red4[1, 0:4] = ring_total(1, 0)
    red4[1, 4:8] = ring_total(1, 1)
    part0 = [put(red4.at[0, :, rem(y + o, NY)], slot_y.at[o - 1], in_y(o)) for o in range(1, NY)]
    part1 = [put(red4.at[1, :, rem(x + o, NX)], slot_x.at[o - 1], in_x(o)) for o in range(1, NX)]
    normed_grad(1)
    ring_step(2, 3)
    n_there = put(gnb.at[other], gnx, partner)

    ring_step(2, 4)
    red8[0:2] = ring_total(2, 0)
    red8[2:4] = ring_total(2, 1)
    part2 = [put(red8.at[rem(x + o, NX)], slot_2x.at[o - 1], in_x(o)) for o in range(1, NX)]

    n_there.wait_recv()
    f_there.wait_recv()
    r_there.wait_recv()
    gsum[...] = jnp.zeros((8, 128), F32)

    def finish_rows(i, carry):
        own = pl.ds(pl.multiple_of(i * 32, 32), 32)
        at = pl.ds(pl.multiple_of(CHIP0 + core * OWN + i * 32, 16), 32)
        inverse = inv_ref[at, :]
        v, vp = xe[at, :].astype(F32), xp[at, :].astype(F32)
        gn = gnb[core, 0, own, :] + gnx[0, own, :]
        gr = gnb[core, 1, own, :] + gnx[1, own, :]
        term = gn * v * inverse + gr * vp * inverse
        cube = inverse * inverse * inverse
        sf, sr = gn * gain[...], gr * gain[...]
        grad_f = 0.5 * ce[at, :].astype(F32) + inverse * sf - v * (cube * jnp.mean(sf * v, -1, keepdims=True))
        grad_r = 0.5 * cp[at, :].astype(F32) + inverse * sr - vp * (cube * jnp.mean(sr * vp, -1, keepdims=True))
        back = dot(grad_r.astype(BF), perm[...])
        grad_ref[own, :] = (grad_f + back).astype(BF)
        mine_f, mine_r = resf[at, :], resr[at, :]
        their_f, their_r = rfx[own, :], rrx[own, :]
        low = core == 0
        full_f = jnp.concatenate(
            [jnp.where(low, mine_f, their_f), jnp.where(low, their_f, mine_f)], axis=1
        )
        mr, tr = mine_r.astype(F32), their_r.astype(F32)
        full_r = jnp.concatenate([jnp.where(low, mr, tr), jnp.where(low, tr, mr)], axis=1)
        back_r = dot(full_r.astype(BF), perm[...])
        out_ref[own, :] = (0.5 * (full_f + back_r)).astype(BF)
        return carry + jnp.sum(term, 0, keepdims=True)

    gain_part = lax.fori_loop(0, OWN // 32, finish_rows, jnp.zeros((1, C), F32))
    for j in range(C // 128):
        gsum[j : j + 1, :] = gain_part[:, j * 128 : (j + 1) * 128]
    to_z = [put(gsum, gz.at[o - 1], in_z(o)) for o in range(1, NZ)]

    def gathered(own, slots):
        total = own
        for o in range(len(slots)):
            total = total + slots[o]
        return total

    for copy in part0 + part1:
        copy.wait_recv()
    one01[:, 0] = gathered(
        red4[0, :, y].astype(F32), [slot_y[o].astype(F32) for o in range(NY - 1)]
    ).astype(BF)
    one01[:, 1] = gathered(
        red4[1, :, x].astype(F32), [slot_x[o].astype(F32) for o in range(NX - 1)]
    ).astype(BF)
    last01 = [put(one01.at[rem(z + o, NZ)], slot_z.at[o - 1], in_z(o)) for o in range(1, NZ)]

    for copy in part2:
        copy.wait_recv()
    one2[...] = gathered(
        red8[x].astype(F32), [slot_2x[o].astype(F32) for o in range(NX - 1)]
    ).astype(BF)
    last2 = [put(one2.at[rem(y + o, NY)], slot_2y.at[o - 1], in_y(o)) for o in range(1, NY)]

    for copy in to_z:
        copy.wait_recv()
    gp_[0] = gathered(gsum[...], [gz[o] for o in range(NZ - 1)])
    to_x = [put(gp_.at[0], gx.at[o - 1], in_x(o)) for o in range(1, NX)]

    for copy in last2:
        copy.wait_recv()
    fin[:, 256:384] = gathered(
        one2[y].astype(F32), [slot_2y[o].astype(F32) for o in range(NY - 1)]
    )
    for copy in to_x:
        copy.wait_recv()
    gp_[1] = gathered(gp_[0], [gx[o] for o in range(NX - 1)])
    to_y = [put(gp_.at[1], gy.at[o - 1], in_y(o)) for o in range(1, NY)]
    for copy in last01:
        copy.wait_recv()
    for j in (0, 1):
        fin[:, j * 128 : (j + 1) * 128] = gathered(
            one01[z, j].astype(F32), [slot_z[o, j].astype(F32) for o in range(NZ - 1)]
        )
    theirs16 = pl.ds(pl.multiple_of(other * 16, 16), 16)
    fin_there = put(fin.at[theirs16], finx, partner)
    for copy in to_y:
        copy.wait_recv()
    gp_[2] = gathered(gp_[1], [gy[o] for o in range(NY - 1)])
    gain_there = put(gp_.at[2], gp_.at[3], partner)
    gk_ref[:, half_cols] = fin[mine16, :]
    fin_there.wait_recv()
    gk_ref[:, other_cols] = finx[...]
    gain_there.wait_recv()
    total = gp_[2] + gp_[3]
    flat = iota((8, 128), 0) * 128 + iota((8, 128), 1)
    picked = jnp.zeros((8, 128), F32)
    for j in range(3):
        chosen = jnp.where(flat == (s * 8 + d) * 3 + j, total, 0.0)
        value = jnp.sum(jnp.sum(chosen, 1, keepdims=True), 0, keepdims=True)
        picked = jnp.where(iota((8, 128), 1) == j, value, picked)
    gg_ref[...] = picked

    for copy in started:
        copy.wait_send()
    for copy in edges:
        copy.wait_send()


def scratch():
    v = pltpu.VMEM
    dma = pltpu.SemaphoreType.DMA
    return [
        v((ROWS, C), BF), v((ROWS, C), BF), v((ROWS, C), BF), v((ROWS, C), BF),
        v((C, C), BF), v((C, HALF), BF), v((ROWS, 1), F32),
        v((2, ROWS + 16, C), F32), v((2 * ROWS, TAPS * C + 128), BF),
        v((2 * ROWS, 4096), BF), v((4096, 512), BF),
        v((3, NZ, NX, NY, 32, 128), BF), v((3, NZ, NX, NY, 32, 128), BF),
        v((2 * ROWS, HALF), F32), v((ROWS, HALF), F32), v((ROWS, HALF), BF),
        v((2, ROWS + 16, HALF), F32), v((2, ROWS, HALF), BF),
        v((TAPS * C, HALF), BF),
        v((2, 2, OWN, C), F32), v((2, OWN, C), F32),
        v((OWN, HALF), F32), v((OWN, HALF), BF),
        v((2, 4, 2, 4, 4, 32, 128), BF), v((4, 4, 2, NY, 32, 128), BF),
        v((2, NZ, 4, 32, 128), BF), v((NX, NY, 32, 128), BF),
        v((3, NZ, 32, 128), BF), v((3, NZ, 32, 128), BF),
        v((3, NY, 32, 128), BF),
        v((NZ, 2, 32, 128), BF), v((NY, 32, 128), BF),
        v((7, 2, 32, 128), BF), v((3, 32, 128), BF),
        v((8, 128), F32), v((7, 8, 128), F32), v((3, 8, 128), F32), v((3, 8, 128), F32),
        v((4, 8, 128), F32),
        v((32, HALF), F32), v((16, HALF), F32),
        dma((MSGS,)), dma((MSGS,)), dma((3,)), dma((6, 2)),
    ]


def per_device(activations, cotangent, weights, norm_gain, pairing):
    padded = jnp.pad(weights, ((0, 1), (0, 0))).reshape(16, 2, 3, 128).transpose(1, 2, 0, 3)
    vmem = pl.BlockSpec(memory_space=pltpu.VMEM)
    anywhere = pl.BlockSpec(memory_space=pl.ANY)
    combined, grad_input, grad_kernel, grad_gain = pl.pallas_call(
        kernel,
        out_shape=(
            jax.ShapeDtypeStruct((OWN, C), BF),
            jax.ShapeDtypeStruct((OWN, C), BF),
            jax.ShapeDtypeStruct((16, C), F32),
            jax.ShapeDtypeStruct((8, 128), F32),
        ),
        in_specs=[anywhere, anywhere, vmem, vmem, vmem],
        out_specs=(vmem, vmem, vmem, vmem),
        scratch_shapes=scratch(),
        compiler_params=pltpu.CompilerParams(
            collective_id=0, has_side_effects=True, vmem_limit_bytes=60 * 2**20
        ),
        name="strands",
    )(activations, cotangent, padded, norm_gain.reshape(1, C), pairing.reshape(1, C))
    return combined[None], grad_input[None], grad_kernel[:15], grad_gain[0, :3]


def solution(mesh):
    placed = (P("dp", "seq", None), P("dp", "seq", None), P(("seq", "dp"), None), P(), P())
    return jax.shard_map(
        per_device,
        mesh=mesh,
        in_specs=placed,
        out_specs=(
            P("dp", "seq", None),
            P("dp", "seq", None),
            P(("seq", "dp"), None),
            P(("seq", "dp")),
        ),
        check_vma=False,
    )
```

```python
import functools

import jax
import jax.numpy as jnp
from jax import lax
from jax.experimental import pallas as pl
from jax.experimental.pallas import tpu as pltpu
from jax.sharding import PartitionSpec as P

EPS = 1e-06
MESH = pl.DeviceIdType.MESH
BF = jnp.bfloat16
F32 = jnp.float32

C = 768
HALF = 384
OWN = 128
TAPS = 5
ROWS = 288
CHIP0 = 16
NZ, NX, NY = 8, 4, 4
MSGS = 128
PHASES = 112


def rem(a, n):
    return lax.rem(a, jnp.int32(n))


def div(a, n):
    return lax.div(a, jnp.int32(n))


def place(z, x, y, c):
    return (z * 4 + div(x, 2) * 2 + c, rem(x, 2) * 4 + y)


def loop(count, body):
    def step(i, carry):
        body(i)
        return carry

    lax.fori_loop(0, count, step, 0)


def dot(a, b):
    return jnp.dot(a, b, preferred_element_type=F32)


def dot_nt(a, b):
    return lax.dot_general(a, b, (((1,), (1,)), ((), ())), preferred_element_type=F32)


def gelu_parts(x):
    k = 0.7978845608028654
    x2 = x * x
    t = jnp.tanh(k * (x + 0.044715 * x2 * x))
    cdf = 0.5 * (1.0 + t)
    slope = cdf + x * (0.5 * (1.0 - t * t)) * (k * (1.0 + 3 * 0.044715 * x2))
    return x * cdf, slope


def kernel(
    act, cot, wshard, gain, pairing,
    out_ref, grad_ref, gk_ref, gg_ref,
    xe, ce, xp, cp, perm, inv_ref, nf, wnd, wp, wpt, wb, dwb, acc,
    resf, resr, gpf, gpb, wun, gnb, gnx, rfx, rrx,
    slot4, slot8, red4, red8, slot_y, slot_x, slot_2x, one01, one2, slot_z, slot_2y,
    gsum, gz, gx, gy, gp_, fin, finx, spread, gather, same, wpad, wsh,
    send, recv, local, halo,
):
    s = lax.axis_index("seq")
    d = lax.axis_index("dp")
    z, xh, core = div(s, 4), rem(div(s, 2), 2), rem(s, 2)
    xl, y = div(d, 4), rem(d, 4)
    x = xh * 2 + xl
    m = z * 2 + xh
    other = 1 - core
    near = div(z, 4) * 4
    far = 4 - near

    def in_x(o):
        return place(z, rem(x + o, NX), y, core)

    def in_y(o):
        return place(z, x, rem(y + o, NY), core)

    def in_z(o):
        return place(rem(z + o, NZ), x, y, core)

    partner = place(z, x, y, other)

    def chip_m(mm, c):
        return place(div(mm, 2), rem(mm, 2) * 2 + xl, y, c)

    def iota(shape, axis):
        return lax.broadcasted_iota(jnp.int32, shape, axis)

    def onehot(flag):
        return flag.astype(F32).astype(BF)

    barrier = pltpu.get_barrier_semaphore()
    met = [partner]
    met += [in_x(o) for o in range(1, NX)] + [in_y(o) for o in range(1, NY)]
    met += [in_z(o) for o in range(1, NZ)]
    met += [chip_m(rem(m + o, 16), c) for o in (1, 15) for c in (0, 1)]
    for who in met:
        pl.semaphore_signal(barrier, inc=1, device_id=who, device_id_type=MESH)

    started = []

    def put(src, dst, who):
        i = len(started)
        copy = pltpu.make_async_remote_copy(
            src_ref=src, dst_ref=dst, send_sem=send.at[i], recv_sem=recv.at[i],
            device_id=who, device_id_type=MESH,
        )
        copy.start()
        started.append(copy)
        return copy

    def keep(src, dst, i):
        copy = pltpu.make_async_copy(src, dst, local.at[i])
        copy.start()
        return copy

    mine16 = pl.ds(pl.multiple_of(core * 16, 16), 16)
    mine = pl.ds(pl.multiple_of(CHIP0 + core * OWN, 16), OWN)
    half_cols = pl.ds(pl.multiple_of(core * HALF, 128), HALF)
    other_cols = pl.ds(pl.multiple_of(other * HALF, 128), HALF)

    x_here = keep(act.at[0], xe.at[mine], 1)
    c_here = keep(cot.at[0], ce.at[mine], 2)

    wpad[0:15, :] = wshard[...].astype(F32)
    wpad[15:16, :] = jnp.zeros((1, C), F32)
    for h in range(2):
        for j in range(3):
            first = h * HALF + j * 128
            wsh[h, j] = wpad[:, first : first + 128].astype(BF)

    perm[...] = onehot(iota((C, C), 0) == pairing[...])

    def source_of(slot):
        r = slot & 15
        c, yy, xx = (slot >> 4) & 1, (slot >> 5) & 3, slot >> 7
        return jnp.where(r < 15, ((c * 2 + xx) * 4 + yy) * 15 + r, -PHASES)

    spread[...] = onehot(iota((PHASES + 384, 256), 0) == source_of(iota((PHASES + 384, 256), 1)) + PHASES)
    gather[...] = onehot(iota((240, 256), 0) == source_of(iota((240, 256), 1)))
    same[...] = onehot(iota((256, 256), 0) == iota((256, 256), 1))
    nf[:, 0:8, :] = jnp.zeros((2, 8, C), F32)
    nf[:, 8 + ROWS :, :] = jnp.zeros((2, 8, C), F32)
    wnd[:, TAPS * C :] = jnp.zeros((2 * ROWS, 128), BF)
    gpf[:, 0:8, :] = jnp.zeros((2, 8, HALF), F32)
    gpf[:, 8 + ROWS :, :] = jnp.zeros((2, 8, HALF), F32)
    gsum[...] = jnp.zeros((8, 128), F32)

    pl.semaphore_wait(barrier, len(met))

    w_there = put(wsh.at[other], wb.at[:, z, x, y, mine16, :], partner)
    w_here = keep(wsh.at[core], wb.at[:, z, x, y, mine16, :], 0)
    edge_src = pl.ds(pl.multiple_of(core * 112, 16), 16)
    edge_dst = pl.ds(pl.multiple_of(other * 272, 16), 16)
    toward = rem(m + core * 2 + 15, 16)
    edges = []
    for c in (0, 1):
        for k, (src, dst) in enumerate(((act, xe), (cot, ce))):
            i = len(edges)
            copy = pltpu.make_async_remote_copy(
                src_ref=src.at[0, edge_src], dst_ref=dst.at[edge_dst],
                send_sem=halo.at[2 + i, 0], recv_sem=halo.at[k, core],
                device_id=chip_m(toward, c), device_id_type=MESH,
            )
            copy.start()
            edges.append(copy)
    x_there = put(act.at[0], xe.at[mine], partner)
    c_there = put(cot.at[0], ce.at[mine], partner)

    todo = []

    def fill(count):
        for _ in range(min(count, len(todo))):
            todo.pop(0)()

    def later(count, pieces, body):
        each = count // pieces
        for k in range(pieces):
            todo.append(lambda k=k: loop(each, lambda i: body(i + k * each)))

    def inside(first, count, width):
        row = iota((count, width), 0) + first
        low = jnp.where(m > 0, 0, CHIP0)
        high = jnp.where(m < 15, ROWS, ROWS - 16)
        return (row >= low) & (row < high)

    def swap_x():
        xp[...] = dot(xe[...], perm[...]).astype(BF)

    def swap_c():
        cp[...] = dot(ce[...], perm[...]).astype(BF)

    def norm_rows(i):
        at = pl.ds(pl.multiple_of(i * 32, 32), 32)
        live_rows = inside(i * 32, 32, C)
        values = jnp.where(live_rows, xe[at, :].astype(F32), 0.0)
        swapped = jnp.where(live_rows, xp[at, :].astype(F32), 0.0)
        inverse = lax.rsqrt(jnp.mean(values * values, -1, keepdims=True) + EPS)
        inv_ref[at, :] = inverse
        into = pl.ds(pl.multiple_of(8 + i * 32, 8), 32)
        nf[0, into, :] = (values * inverse * gain[...]).astype(BF).astype(F32)
        nf[1, into, :] = (swapped * inverse * gain[...]).astype(BF).astype(F32)

    def window_cols(i):
        cols = pl.ds(pl.multiple_of(i * 128, 128), 128)
        for strand in (0, 1):
            for k in range(TAPS):
                shift = (k - 2) if strand == 0 else (2 - k)
                into = pl.ds(pl.multiple_of(k * C + i * 128, 128), 128)
                wnd[strand * ROWS : (strand + 1) * ROWS, into] = nf[
                    strand, 8 + shift : 8 + shift + ROWS, cols
                ].astype(BF)

    def pad_group(g):
        cols = pl.ds(pl.multiple_of(div(15 * g, 8) * 128, 128), 384)
        right = spread[pl.ds(pl.multiple_of(PHASES - 16 * rem(15 * g, 8), 16), 384), :]
        into = pl.ds(pl.multiple_of(g * 256, 256), 256)
        wp[:, into] = dot(wnd[:, cols], right).astype(BF)

    def pad_group_t(g):
        at = pl.ds(pl.multiple_of(g * 256, 256), 256)
        for strand in (0, 1):
            rows = slice(strand * ROWS + CHIP0, strand * ROWS + CHIP0 + 256)
            wpt[at, strand * 256 : (strand + 1) * 256] = dot_nt(same[...], wp[rows, at]).astype(BF)

    todo.append(swap_x)
    todo.append(swap_c)
    later(9, 3, norm_rows)
    later(6, 3, window_cols)
    later(16, 8, pad_group)
    later(16, 8, pad_group_t)

    w_here.wait()
    w_there.wait_recv()
    first01 = [
        put(wb.at[pl.ds(0, 2), z, x, y], wb.at[pl.ds(0, 2), z, x, y], in_z(o)) for o in (4, 3, 5, 2, 6, 1, 7)
    ]
    first2 = [put(wb.at[2, z, x, y], wb.at[2, z, x, y], in_y(o)) for o in range(1, NY)]

    x_here.wait()
    c_here.wait()
    x_there.wait_recv()
    c_there.wait_recv()
    for copy in first2:
        copy.wait_recv()
    second2 = [put(wb.at[2, z, x], wb.at[2, z, x], in_x(o)) for o in range(1, NX)]
    for k, dst in enumerate((xe, ce)):
        for side in (0, 1):
            into = dst.at[pl.ds(272 * (1 - side), 16)]
            pltpu.make_async_remote_copy(
                src_ref=into, dst_ref=into, send_sem=halo.at[2, 0], recv_sem=halo.at[k, side],
                device_id=partner, device_id_type=MESH,
            ).wait_recv()

    def part(ref, colour, coord, half):
        if colour == 2:
            return ref.at[2, coord, pl.ds(half * 2, 2)]
        planes = pl.ds(far if half == 0 else near, 4)
        return ref.at[0, planes, coord] if colour == 0 else ref.at[1, planes, :, coord]

    rings = ((x, NX, in_x), (y, NY, in_y), (z, NZ, in_z))
    ways = ((1, 0), (-1, 1), (1, 1), (-1, 0))

    def limit(n, sign, half):
        return n // 2 if (half == 0) == (sign == 1) else n // 2 - 1

    def ring_send(colour, sign, half, hop):
        q, n, who = rings[colour]
        held = part(wb, colour, rem(q - sign * (hop - 1) + n, n), half)
        return put(held, held, who(1 if sign == 1 else n - 1))

    live = {}

    def ring_start(colour):
        for sign, half in ways:
            live[colour, sign, half] = ring_send(colour, sign, half, 1)

    def ring_hop(colour, hop, pieces):
        n = rings[colour][1]
        for sign, half in ways:
            if hop > limit(n, sign, half):
                continue
            live[colour, sign, half].wait_recv()
            if hop < limit(n, sign, half):
                live[colour, sign, half] = ring_send(colour, sign, half, hop + 1)
            fill(pieces)

    fill(1)
    for copy in first01:
        copy.wait_recv()
    second0 = [put(wb.at[0, :, x, y], wb.at[0, :, x, y], in_y(o)) for o in range(1, NY)]
    second1 = [put(wb.at[1, :, x, y], wb.at[1, :, x, y], in_x(o)) for o in range(1, NX)]
    fill(1)
    for copy in second2:
        copy.wait_recv()
    ring_start(2)
    fill(5)
    for copy in second0:
        copy.wait_recv()
    ring_start(0)
    for copy in second1:
        copy.wait_recv()
    ring_start(1)
    fill(4)
    ring_hop(2, 1, 0)
    fill(1)
    ring_hop(2, 2, 0)
    ring_hop(0, 1, 0)
    ring_hop(1, 1, 0)
    fill(2)
    ring_hop(2, 3, 1)
    fill(len(todo))
    ring_hop(0, 2, 0)
    ring_hop(1, 2, 0)
    ring_hop(2, 4, 0)

    def right_of(zz, count):
        return jnp.concatenate(
            [wb[j, pl.ds(zz, count)].reshape(count * 512, 128) for j in range(3)], axis=1
        )

    def left_of(zz, count):
        return wp[:, pl.ds(pl.multiple_of(zz * 512, 512), count * 512)]

    acc[...] = dot(left_of(0, 2), right_of(0, 2))

    def forward_step(i):
        acc[...] += dot(left_of(i * 2 + 2, 2), right_of(i * 2 + 2, 2))

    loop(3, forward_step)

    def gelu_rows(strand):
        def body(i):
            at = pl.ds(pl.multiple_of(i * 32, 32), 32)
            pre = acc[pl.ds(pl.multiple_of(strand * ROWS + i * 32, 32), 32), :]
            value, slope = gelu_parts(pre)
            if strand == 0:
                resf[at, :] = xe[at, half_cols].astype(F32) + value
                g = ce[at, half_cols].astype(F32)
            else:
                resr[at, :] = (xp[at, half_cols].astype(F32) + value).astype(BF)
                g = cp[at, half_cols].astype(F32)
            gp = jnp.where(inside(i * 32, 32, HALF), 0.5 * g * slope, 0.0).astype(BF)
            gpb[strand, at, :] = gp
            gpf[strand, pl.ds(pl.multiple_of(8 + i * 32, 8), 32), :] = gp.astype(F32)

        return body

    loop(ROWS // 32, gelu_rows(0))
    loop(ROWS // 32, gelu_rows(1))

    def dw_pair(p):
        right = jnp.concatenate(
            [gpb[0, CHIP0 : CHIP0 + 256, :], gpb[1, CHIP0 : CHIP0 + 256, :]], axis=0
        )
        got = dot(wpt[pl.ds(pl.multiple_of(p * 1024, 1024), 1024), :], right).astype(BF)
        for j in range(3):
            dwb[j, pl.ds(p * 2, 2)] = got[:, j * 128 : (j + 1) * 128].reshape(2, NX, NY, 32, 128)

    def ring_slot(colour, sign, half, dist):
        way = ways.index((sign, half))
        if colour == 2:
            return slot8.at[way, dist - 1]
        return slot4.at[colour, way, dist - 1]

    def ring_give(colour, sign, half, dist, src):
        q, n, who = rings[colour]
        return put(src, ring_slot(colour, sign, half, dist), who(1 if sign == 1 else n - 1))

    def ring_open(colour, sign, half):
        q, n, who = rings[colour]
        dist = limit(n, sign, half)
        src = part(dwb, colour, rem(q + sign * dist + n, n), half)
        live[colour, sign, half] = ring_give(colour, sign, half, dist, src)

    own_pair = div(z, 2)
    far_pair = rem(own_pair + 2, 4)
    dw_pair(far_pair)
    ring_open(2, 1, 0)
    ring_open(2, -1, 1)
    dw_pair(far_pair + 1 - 2 * rem(far_pair, 2))
    for colour in (0, 1):
        ring_open(colour, 1, 0)
        ring_open(colour, -1, 0)
    dw_pair(own_pair + 1 - 2 * rem(own_pair, 2))
    dw_pair(own_pair)
    ring_open(2, 1, 1)
    ring_open(2, -1, 0)
    for colour in (0, 1):
        ring_open(colour, 1, 1)
        ring_open(colour, -1, 1)

    there = pl.ds(pl.multiple_of(CHIP0 + other * OWN, 16), OWN)
    f_there = put(resf.at[there], rfx, partner)
    r_there = put(resr.at[there], rrx, partner)

    def pack_group(g):
        zz, hh = div(g, 2), rem(g, 2) * 2
        right = jnp.concatenate(
            [wb[j, zz, pl.ds(hh, 2)].reshape(256, 128) for j in range(3)], axis=1
        )
        wun[pl.ds(pl.multiple_of(g * 240, 16), 240), :] = dot(gather[...], right).astype(BF)

    def normed_grad(block, strand):
        first = 8 + CHIP0 + block * OWN
        total = None
        for k in range(TAPS):
            shift = (2 - k) if strand == 0 else (k - 2)
            left = gpf[strand, first + shift : first + shift + OWN, :].astype(BF)
            term = dot_nt(left, wun[k * C : (k + 1) * C, :])
            total = term if total is None else total + term
        gnb[block, strand] = total

    later(16, 4, pack_group)
    for block in (0, 1):
        for strand in (0, 1):
            todo.append(functools.partial(normed_grad, block, strand))

    def give_normed():
        live["gn"] = put(gnb.at[other], gnx, partner)

    todo.append(give_normed)

    def ring_step(colour, hop, pieces):
        q, n, who = rings[colour]
        for sign, half in ways:
            dist = limit(n, sign, half) - (hop - 1)
            if dist < 1:
                continue
            live[colour, sign, half].wait_recv()
            if dist > 1:
                got = ring_slot(colour, sign, half, dist)
                add = part(dwb, colour, rem(q + sign * (dist - 1) + n, n), half)
                got[...] = (got[...].astype(F32) + add[...].astype(F32)).astype(BF)
                live[colour, sign, half] = ring_give(colour, sign, half, dist - 1, got)
            fill(pieces)

    def ring_total(colour, half):
        q = rings[colour][0]
        total = part(dwb, colour, q, half)[...].astype(F32)
        for sign in (1, -1):
            total = total + ring_slot(colour, sign, half, 1)[...].astype(F32)
        return total.astype(BF)

    def finish_gain():
        live["gn"].wait_recv()
        at = mine
        inverse = inv_ref[at, :]
        v, vp = xe[at, :].astype(F32), xp[at, :].astype(F32)
        gn = gnb[core, 0] + gnx[0]
        gr = gnb[core, 1] + gnx[1]
        gnb[core, 0] = gn
        gnb[core, 1] = gr
        gain_part = jnp.sum(gn * v * inverse + gr * vp * inverse, 0, keepdims=True)
        for j in range(C // 128):
            gsum[j : j + 1, :] = gain_part[:, j * 128 : (j + 1) * 128]
        live["to_z"] = [put(gsum, gz.at[o - 1], in_z(o)) for o in range(1, NZ)]

    def finish_grad():
        at = mine
        inverse = inv_ref[at, :]
        cube = inverse * inverse * inverse
        v, vp = xe[at, :].astype(F32), xp[at, :].astype(F32)
        sf, sr = gnb[core, 0] * gain[...], gnb[core, 1] * gain[...]
        grad_r = 0.5 * cp[at, :].astype(F32) + inverse * sr - vp * (cube * jnp.mean(sr * vp, -1, keepdims=True))
        back = dot(grad_r.astype(BF), perm[...])
        grad_f = 0.5 * ce[at, :].astype(F32) + inverse * sf - v * (cube * jnp.mean(sf * v, -1, keepdims=True))
        grad_ref[...] = (grad_f + back).astype(BF)

    def finish_out():
        f_there.wait_recv()
        r_there.wait_recv()
        low = core == 0
        mine_f, their_f = resf[mine, :], rfx[...]
        mr, tr = resr[mine, :].astype(F32), rrx[...].astype(F32)
        full_r = jnp.concatenate([jnp.where(low, mr, tr), jnp.where(low, tr, mr)], axis=1)
        back_r = dot(full_r.astype(BF), perm[...])
        full_f = jnp.concatenate(
            [jnp.where(low, mine_f, their_f), jnp.where(low, their_f, mine_f)], axis=1
        )
        out_ref[...] = (0.5 * (full_f + back_r)).astype(BF)

    todo.append(finish_out)
    todo.append(finish_gain)
    todo.append(finish_grad)

    def gathered(own, slots):
        total = own
        for one in slots:
            total = total + one
        return total

    fill(5)
    ring_step(2, 1, 0)
    fill(1)
    ring_step(0, 1, 0)
    ring_step(1, 1, 0)
    fill(1)
    ring_step(2, 2, 0)
    fill(2)
    ring_step(0, 2, 0)
    ring_step(1, 2, 0)
    planes = (pl.ds(far, 4), pl.ds(near, 4))
    for colour in (0, 1):
        for half in (0, 1):
            red4[colour, planes[half]] = ring_total(colour, half)
    part0 = [put(red4.at[0, :, rem(y + o, NY)], slot_y.at[o - 1], in_y(o)) for o in range(1, NY)]
    part1 = [put(red4.at[1, :, rem(x + o, NX)], slot_x.at[o - 1], in_x(o)) for o in range(1, NX)]
    ring_step(2, 3, 0)
    fill(2)
    ring_step(2, 4, 0)
    red8[0:2] = ring_total(2, 0)
    red8[2:4] = ring_total(2, 1)
    part2 = [put(red8.at[rem(x + o, NX)], slot_2x.at[o - 1], in_x(o)) for o in range(1, NX)]
    fill(len(todo))

    for copy in part0 + part1:
        copy.wait_recv()
    one01[:, 0] = gathered(
        red4[0, :, y].astype(F32), [slot_y[o].astype(F32) for o in range(NY - 1)]
    ).astype(BF)
    one01[:, 1] = gathered(
        red4[1, :, x].astype(F32), [slot_x[o].astype(F32) for o in range(NX - 1)]
    ).astype(BF)
    last01 = [
        put(one01.at[rem(z + o, NZ)], slot_z.at[o - 1], in_z(o)) for o in (4, 3, 5, 2, 6, 1, 7)
    ]

    for copy in live["to_z"]:
        copy.wait_recv()
    gp_[0] = gathered(gsum[...], [gz[o] for o in range(NZ - 1)])
    to_x = [put(gp_.at[0], gx.at[o - 1], in_x(o)) for o in range(1, NX)]

    for copy in part2:
        copy.wait_recv()
    one2[...] = gathered(
        red8[x].astype(F32), [slot_2x[o].astype(F32) for o in range(NX - 1)]
    ).astype(BF)
    last2 = [put(one2.at[rem(y + o, NY)], slot_2y.at[o - 1], in_y(o)) for o in range(1, NY)]

    for copy in to_x:
        copy.wait_recv()
    gp_[1] = gathered(gp_[0], [gx[o] for o in range(NX - 1)])
    to_y = [put(gp_.at[1], gy.at[o - 1], in_y(o)) for o in range(1, NY)]
    for copy in last2:
        copy.wait_recv()
    fin[:, 256:384] = gathered(
        one2[y].astype(F32), [slot_2y[o].astype(F32) for o in range(NY - 1)]
    )
    for copy in last01:
        copy.wait_recv()
    for j in (0, 1):
        fin[:, j * 128 : (j + 1) * 128] = gathered(
            one01[z, j].astype(F32), [slot_z[o, j].astype(F32) for o in range(NZ - 1)]
        )
    theirs16 = pl.ds(pl.multiple_of(other * 16, 16), 16)
    fin_there = put(fin.at[theirs16], finx, partner)
    for copy in to_y:
        copy.wait_recv()
    gp_[2] = gathered(gp_[1], [gy[o] for o in range(NY - 1)])
    gain_there = put(gp_.at[2], gp_.at[3], partner)
    gk_ref[:, half_cols] = fin[mine16, :]
    fin_there.wait_recv()
    gk_ref[:, other_cols] = finx[...]
    gain_there.wait_recv()
    total = gp_[2] + gp_[3]
    flat = iota((8, 128), 0) * 128 + iota((8, 128), 1)
    picked = jnp.zeros((8, 128), F32)
    for j in range(3):
        chosen = jnp.where(flat == (s * 8 + d) * 3 + j, total, 0.0)
        value = jnp.sum(jnp.sum(chosen, 1, keepdims=True), 0, keepdims=True)
        picked = jnp.where(iota((8, 128), 1) == j, value, picked)
    gg_ref[...] = picked

    for copy in started:
        copy.wait_send()
    for copy in edges:
        copy.wait_send()


def scratch():
    v = pltpu.VMEM
    dma = pltpu.SemaphoreType.DMA
    return [
        v((ROWS, C), BF), v((ROWS, C), BF), v((ROWS, C), BF), v((ROWS, C), BF),
        v((C, C), BF), v((ROWS, 1), F32),
        v((2, ROWS + 16, C), F32), v((2 * ROWS, TAPS * C + 128), BF),
        v((2 * ROWS, 4096), BF), v((4096, 512), BF),
        v((3, NZ, NX, NY, 32, 128), BF), v((3, NZ, NX, NY, 32, 128), BF),
        v((2 * ROWS, HALF), F32), v((ROWS, HALF), F32), v((ROWS, HALF), BF),
        v((2, ROWS + 16, HALF), F32), v((2, ROWS, HALF), BF),
        v((TAPS * C, HALF), BF),
        v((2, 2, OWN, C), F32), v((2, OWN, C), F32),
        v((OWN, HALF), F32), v((OWN, HALF), BF),
        v((2, 4, 2, 4, 4, 32, 128), BF), v((4, 4, 2, NY, 32, 128), BF),
        v((2, NZ, 4, 32, 128), BF), v((NX, NY, 32, 128), BF),
        v((3, NZ, 32, 128), BF), v((3, NZ, 32, 128), BF),
        v((3, NY, 32, 128), BF),
        v((NZ, 2, 32, 128), BF), v((NY, 32, 128), BF),
        v((7, 2, 32, 128), BF), v((3, 32, 128), BF),
        v((8, 128), F32), v((7, 8, 128), F32), v((3, 8, 128), F32), v((3, 8, 128), F32),
        v((4, 8, 128), F32),
        v((32, HALF), F32), v((16, HALF), F32),
        v((PHASES + 384, 256), BF), v((240, 256), BF), v((256, 256), BF),
        v((16, C), F32), v((2, 3, 16, 128), BF),
        dma((MSGS,)), dma((MSGS,)), dma((3,)), dma((6, 2)),
    ]


def per_device(activations, cotangent, weights, norm_gain, pairing):
    vmem = pl.BlockSpec(memory_space=pltpu.VMEM)
    anywhere = pl.BlockSpec(memory_space=pl.ANY)
    combined, grad_input, grad_kernel, grad_gain = pl.pallas_call(
        kernel,
        out_shape=(
            jax.ShapeDtypeStruct((OWN, C), BF),
            jax.ShapeDtypeStruct((OWN, C), BF),
            jax.ShapeDtypeStruct((16, C), F32),
            jax.ShapeDtypeStruct((8, 128), F32),
        ),
        in_specs=[anywhere, anywhere, vmem, vmem, vmem],
        out_specs=(vmem, vmem, vmem, vmem),
        scratch_shapes=scratch(),
        compiler_params=pltpu.CompilerParams(
            collective_id=0, has_side_effects=True, vmem_limit_bytes=60 * 2**20
        ),
        name="strands",
    )(activations, cotangent, weights, norm_gain.reshape(1, C), pairing.reshape(1, C))
    return combined[None], grad_input[None], grad_kernel[:15], grad_gain[0, :3]


def solution(mesh):
    placed = (P("dp", "seq", None), P("dp", "seq", None), P(("seq", "dp"), None), P(), P())
    return jax.shard_map(
        per_device,
        mesh=mesh,
        in_specs=placed,
        out_specs=(
            P("dp", "seq", None),
            P("dp", "seq", None),
            P(("seq", "dp"), None),
            P(("seq", "dp")),
        ),
        check_vma=False,
    )
```

```python
import functools

import jax
import jax.numpy as jnp
from jax import lax
from jax.experimental import pallas as pl
from jax.experimental.pallas import tpu as pltpu
from jax.sharding import PartitionSpec as P

EPS = 1e-06
MESH = pl.DeviceIdType.MESH
BF = jnp.bfloat16
F32 = jnp.float32

C = 768
HALF = 384
OWN = 128
TAPS = 5
ROWS = 288
CHIP0 = 16
NZ, NX, NY = 8, 4, 4
MSGS = 176
PHASES = 112


def rem(a, n):
    return lax.rem(a, jnp.int32(n))


def div(a, n):
    return lax.div(a, jnp.int32(n))


def place(z, x, y, c):
    return (z * 4 + div(x, 2) * 2 + c, rem(x, 2) * 4 + y)


def loop(count, body):
    def step(i, carry):
        body(i)
        return carry

    lax.fori_loop(0, count, step, 0)


def dot(a, b):
    return jnp.dot(a, b, preferred_element_type=F32)


def dot_nt(a, b):
    return lax.dot_general(a, b, (((1,), (1,)), ((), ())), preferred_element_type=F32)


def gelu_parts(x):
    k = 0.7978845608028654
    x2 = x * x
    t = jnp.tanh(k * (x + 0.044715 * x2 * x))
    cdf = 0.5 * (1.0 + t)
    slope = cdf + x * (0.5 * (1.0 - t * t)) * (k * (1.0 + 3 * 0.044715 * x2))
    return x * cdf, slope


def kernel(
    act, cot, wshard, gain, pairing,
    out_ref, grad_ref, gk_ref, gg_ref,
    xe, ce, xp, cp, perm, inv_ref, nf, wnd, wp, wpt, wb, dwb, acc,
    resf, resr, gpf, gpb, wun, gnb, gnx, rfx, rrx,
    slot4, slot8, red4, red8, slot_y, slot_x, slot_2x, one01, one2, slot_z, slot_2y,
    gsum, gz, gx, gy, gp_, fin, finx, spread, gather, wpad, wsh, gain2,
    send, recv, local, halo,
):
    s = lax.axis_index("seq")
    d = lax.axis_index("dp")
    z, xh, core = div(s, 4), rem(div(s, 2), 2), rem(s, 2)
    xl, y = div(d, 4), rem(d, 4)
    x = xh * 2 + xl
    m = z * 2 + xh
    other = 1 - core
    near = div(z, 4) * 4
    far = 4 - near

    def in_x(o):
        return place(z, rem(x + o, NX), y, core)

    def in_y(o):
        return place(z, x, rem(y + o, NY), core)

    def in_z(o):
        return place(rem(z + o, NZ), x, y, core)

    partner = place(z, x, y, other)

    def chip_m(mm, c):
        return place(div(mm, 2), rem(mm, 2) * 2 + xl, y, c)

    def iota(shape, axis):
        return lax.broadcasted_iota(jnp.int32, shape, axis)

    def onehot(flag):
        return flag.astype(F32).astype(BF)

    barrier = pltpu.get_barrier_semaphore()
    met = [partner]
    met += [in_x(o) for o in range(1, NX)] + [in_y(o) for o in range(1, NY)]
    met += [in_z(o) for o in range(1, NZ)]
    met += [chip_m(rem(m + o, 16), c) for o in (1, 15) for c in (0, 1)]
    for who in met:
        pl.semaphore_signal(barrier, inc=1, device_id=who, device_id_type=MESH)

    started = []

    def put(src, dst, who):
        i = len(started)
        copy = pltpu.make_async_remote_copy(
            src_ref=src, dst_ref=dst, send_sem=send.at[i], recv_sem=recv.at[i],
            device_id=who, device_id_type=MESH,
        )
        copy.start()
        started.append(copy)
        return copy

    def keep(src, dst, i):
        copy = pltpu.make_async_copy(src, dst, local.at[i])
        copy.start()
        return copy

    mine16 = pl.ds(pl.multiple_of(core * 16, 16), 16)
    mine = pl.ds(pl.multiple_of(CHIP0 + core * OWN, 16), OWN)
    half_cols = pl.ds(pl.multiple_of(core * HALF, 128), HALF)
    other_cols = pl.ds(pl.multiple_of(other * HALF, 128), HALF)

    x_here = keep(act.at[0], xe.at[mine], 1)
    c_here = keep(cot.at[0], ce.at[mine], 2)

    wpad[0:15, :] = wshard[...].astype(F32)
    wpad[15:16, :] = jnp.zeros((1, C), F32)
    for h in range(2):
        for j in range(3):
            first = h * HALF + j * 128
            wsh[h, j] = wpad[:, first : first + 128].astype(BF)

    gain_row = gain[...].reshape(1, C)
    perm[...] = onehot(iota((C, C), 0) == pairing[...].reshape(1, C))
    gain2[...] = gain_row

    def source_of(slot):
        r = slot & 15
        c, yy, xx = (slot >> 4) & 1, (slot >> 5) & 3, slot >> 7
        return jnp.where(r < 15, ((c * 2 + xx) * 4 + yy) * 15 + r, -PHASES)

    spread[...] = onehot(iota((PHASES + 384, 256), 0) == source_of(iota((PHASES + 384, 256), 1)) + PHASES)
    gather[...] = onehot(iota((240, 256), 0) == source_of(iota((240, 256), 1)))
    nf[:, 0:8, :] = jnp.zeros((2, 8, C), F32)
    nf[:, 8 + ROWS :, :] = jnp.zeros((2, 8, C), F32)
    wnd[:, TAPS * C :] = jnp.zeros((2 * ROWS, 128), BF)
    gpf[:, 0:8, :] = jnp.zeros((2, 8, HALF), F32)
    gpf[:, 8 + ROWS :, :] = jnp.zeros((2, 8, HALF), F32)
    gsum[...] = jnp.zeros((8, 128), F32)

    pl.semaphore_wait(barrier, len(met))

    w_there = put(wsh.at[other], wb.at[:, z, x, y, mine16, :], partner)
    w_here = keep(wsh.at[core], wb.at[:, z, x, y, mine16, :], 0)
    edge_src = pl.ds(pl.multiple_of(core * 112, 16), 16)
    edge_dst = pl.ds(pl.multiple_of(other * 272, 16), 16)
    toward = rem(m + core * 2 + 15, 16)
    edges = []
    for c in (0, 1):
        for k, (src, dst) in enumerate(((act, xe), (cot, ce))):
            i = len(edges)
            copy = pltpu.make_async_remote_copy(
                src_ref=src.at[0, edge_src], dst_ref=dst.at[edge_dst],
                send_sem=halo.at[2 + i, 0], recv_sem=halo.at[k, core],
                device_id=chip_m(toward, c), device_id_type=MESH,
            )
            copy.start()
            edges.append(copy)
    x_there = put(act.at[0], xe.at[mine], partner)
    c_there = put(cot.at[0], ce.at[mine], partner)

    todo = []

    def fill(count):
        for _ in range(min(count, len(todo))):
            todo.pop(0)()

    def later(count, pieces, body):
        each = count // pieces
        for k in range(pieces):
            todo.append(lambda k=k: loop(each, lambda i: body(i + k * each)))

    def inside(first, count, width):
        row = iota((count, width), 0) + first
        low = jnp.where(m > 0, 0, CHIP0)
        high = jnp.where(m < 15, ROWS, ROWS - 16)
        return (row >= low) & (row < high)

    def swap_x():
        xp[...] = dot(xe[...], perm[...]).astype(BF)

    def swap_c():
        cp[...] = dot(ce[...], perm[...]).astype(BF)

    def norm_rows(i):
        at = pl.ds(pl.multiple_of(i * 32, 32), 32)
        live_rows = inside(i * 32, 32, C)
        values = jnp.where(live_rows, xe[at, :].astype(F32), 0.0)
        swapped = jnp.where(live_rows, xp[at, :].astype(F32), 0.0)
        inverse = lax.rsqrt(jnp.mean(values * values, -1, keepdims=True) + EPS)
        inv_ref[at, :] = inverse
        into = pl.ds(pl.multiple_of(8 + i * 32, 8), 32)
        nf[0, into, :] = (values * inverse * gain2[...]).astype(BF).astype(F32)
        nf[1, into, :] = (swapped * inverse * gain2[...]).astype(BF).astype(F32)

    def window_cols(i):
        cols = pl.ds(pl.multiple_of(i * 128, 128), 128)
        for strand in (0, 1):
            for k in range(TAPS):
                shift = (k - 2) if strand == 0 else (2 - k)
                into = pl.ds(pl.multiple_of(k * C + i * 128, 128), 128)
                wnd[strand * ROWS : (strand + 1) * ROWS, into] = nf[
                    strand, 8 + shift : 8 + shift + ROWS, cols
                ].astype(BF)

    def pad_group(g):
        cols = pl.ds(pl.multiple_of(div(15 * g, 8) * 128, 128), 384)
        right = spread[pl.ds(pl.multiple_of(PHASES - 16 * rem(15 * g, 8), 16), 384), :]
        into = pl.ds(pl.multiple_of(g * 256, 256), 256)
        wp[:, into] = dot(wnd[:, cols], right).astype(BF)

    def pad_group_t(g):
        at = pl.ds(pl.multiple_of(g * 256, 256), 256)
        for strand in (0, 1):
            rows = slice(strand * ROWS + CHIP0, strand * ROWS + CHIP0 + 256)
            wpt[at, strand * 256 : (strand + 1) * 256] = wp[rows, at].T

    todo.append(swap_x)
    todo.append(swap_c)
    later(9, 3, norm_rows)
    later(6, 3, window_cols)
    later(16, 8, pad_group)
    later(16, 8, pad_group_t)

    second0, second1 = {}, {}

    def forward_shard(o):
        zz = rem(z + NZ - o, NZ)
        held0, held1 = wb.at[0, zz, x, y], wb.at[1, zz, x, y]
        second0[o] = [put(held0, held0, in_y(p)) for p in (2, 1, 3)]
        second1[o] = [put(held1, held1, in_x(p)) for p in (2, 1, 3)]

    w_here.wait()
    w_there.wait_recv()
    first2 = [put(wb.at[2, z, x, y], wb.at[2, z, x, y], in_y(o)) for o in (2, 1, 3)]
    first01 = {
        o: put(wb.at[pl.ds(0, 2), z, x, y], wb.at[pl.ds(0, 2), z, x, y], in_z(o))
        for o in (4, 3, 5, 2, 6, 1, 7)
    }
    forward_shard(0)

    def pass_on(*offsets):
        for o in offsets:
            first01[o].wait_recv()
            forward_shard(o)

    def part(ref, colour, coord, half):
        if colour == 2:
            return ref.at[2, coord, pl.ds(half * 2, 2)]
        planes = pl.ds(far if half == 0 else near, 4)
        return ref.at[0, planes, coord] if colour == 0 else ref.at[1, planes, :, coord]

    rings = ((x, NX, in_x), (y, NY, in_y), (z, NZ, in_z))
    ways = ((1, 0), (-1, 1), (1, 1), (-1, 0))

    def limit(n, sign, half):
        return n // 2 if (half == 0) == (sign == 1) else n // 2 - 1

    def ring_send(colour, sign, half, hop):
        q, n, who = rings[colour]
        held = part(wb, colour, rem(q - sign * (hop - 1) + n, n), half)
        return put(held, held, who(1 if sign == 1 else n - 1))

    live = {}

    def ring_start(colour):
        for sign, half in ways:
            live[colour, sign, half] = ring_send(colour, sign, half, 1)

    def ring_hop(colour, hop, pieces):
        n = rings[colour][1]
        for sign, half in ways:
            if hop > limit(n, sign, half):
                continue
            live[colour, sign, half].wait_recv()
            if hop < limit(n, sign, half):
                live[colour, sign, half] = ring_send(colour, sign, half, hop + 1)
            fill(pieces)

    for copy in first2:
        copy.wait_recv()
    second2 = [put(wb.at[2, z, x], wb.at[2, z, x], in_x(o)) for o in (2, 1, 3)]
    pass_on(1, 7)
    x_here.wait()
    c_here.wait()
    x_there.wait_recv()
    c_there.wait_recv()
    pass_on(2, 6)
    for k, dst in enumerate((xe, ce)):
        for side in (0, 1):
            into = dst.at[pl.ds(272 * (1 - side), 16)]
            pltpu.make_async_remote_copy(
                src_ref=into, dst_ref=into, send_sem=halo.at[2, 0], recv_sem=halo.at[k, side],
                device_id=partner, device_id_type=MESH,
            ).wait_recv()
    pass_on(3, 5)
    fill(1)
    pass_on(4)
    for copy in second2:
        copy.wait_recv()
    ring_start(2)
    fill(4)
    for o in (0, 1, 7, 2, 6, 3, 5, 4):
        for copy in second0[o] + second1[o]:
            copy.wait_recv()
    ring_start(0)
    ring_start(1)
    fill(3)
    ring_hop(2, 1, 0)
    fill(3)
    ring_hop(2, 2, 0)
    fill(2)
    ring_hop(0, 1, 0)
    ring_hop(1, 1, 0)
    fill(2)
    ring_hop(2, 3, 0)
    fill(len(todo))
    ring_hop(0, 2, 0)
    ring_hop(1, 2, 0)
    ring_hop(2, 4, 0)

    def right_of(zz, count):
        return jnp.concatenate(
            [wb[j, pl.ds(zz, count)].reshape(count * 512, 128) for j in range(3)], axis=1
        )

    def left_of(zz, count):
        return wp[:, pl.ds(pl.multiple_of(zz * 512, 512), count * 512)]

    acc[...] = dot(left_of(0, 2), right_of(0, 2))

    def forward_step(i):
        acc[...] += dot(left_of(i * 2 + 2, 2), right_of(i * 2 + 2, 2))

    loop(3, forward_step)

    def gelu_rows(strand):
        def body(i):
            at = pl.ds(pl.multiple_of(i * 32, 32), 32)
            pre = acc[pl.ds(pl.multiple_of(strand * ROWS + i * 32, 32), 32), :]
            value, slope = gelu_parts(pre)
            if strand == 0:
                resf[at, :] = xe[at, half_cols].astype(F32) + value
                g = ce[at, half_cols].astype(F32)
            else:
                resr[at, :] = (xp[at, half_cols].astype(F32) + value).astype(BF)
                g = cp[at, half_cols].astype(F32)
            gp = jnp.where(inside(i * 32, 32, HALF), 0.5 * g * slope, 0.0).astype(BF)
            gpb[strand, at, :] = gp
            gpf[strand, pl.ds(pl.multiple_of(8 + i * 32, 8), 32), :] = gp.astype(F32)

        return body

    loop(ROWS // 32, gelu_rows(0))
    loop(ROWS // 32, gelu_rows(1))

    def dw_pair(p):
        right = jnp.concatenate(
            [gpb[0, CHIP0 : CHIP0 + 256, :], gpb[1, CHIP0 : CHIP0 + 256, :]], axis=0
        )
        got = dot(wpt[pl.ds(pl.multiple_of(p * 1024, 1024), 1024), :], right).astype(BF)
        for j in range(3):
            dwb[j, pl.ds(p * 2, 2)] = got[:, j * 128 : (j + 1) * 128].reshape(2, NX, NY, 32, 128)

    def ring_slot(colour, sign, half, dist):
        way = ways.index((sign, half))
        if colour == 2:
            return slot8.at[way, dist - 1]
        return slot4.at[colour, way, dist - 1]

    def ring_give(colour, sign, half, dist, src):
        q, n, who = rings[colour]
        return put(src, ring_slot(colour, sign, half, dist), who(1 if sign == 1 else n - 1))

    def ring_open(colour, sign, half):
        q, n, who = rings[colour]
        dist = limit(n, sign, half)
        src = part(dwb, colour, rem(q + sign * dist + n, n), half)
        live[colour, sign, half] = ring_give(colour, sign, half, dist, src)

    own_pair = div(z, 2)
    far_pair = rem(own_pair + 2, 4)
    dw_pair(far_pair)
    ring_open(2, 1, 0)
    ring_open(2, -1, 1)
    dw_pair(far_pair + 1 - 2 * rem(far_pair, 2))
    for colour in (0, 1):
        ring_open(colour, 1, 0)
        ring_open(colour, -1, 0)
    dw_pair(own_pair + 1 - 2 * rem(own_pair, 2))
    dw_pair(own_pair)
    ring_open(2, 1, 1)
    ring_open(2, -1, 0)
    for colour in (0, 1):
        ring_open(colour, 1, 1)
        ring_open(colour, -1, 1)

    there = pl.ds(pl.multiple_of(CHIP0 + other * OWN, 16), OWN)
    f_there = put(resf.at[there], rfx, partner)
    r_there = put(resr.at[there], rrx, partner)

    def pack_group(g):
        zz, hh = div(g, 2), rem(g, 2) * 2
        right = jnp.concatenate(
            [wb[j, zz, pl.ds(hh, 2)].reshape(256, 128) for j in range(3)], axis=1
        )
        wun[pl.ds(pl.multiple_of(g * 240, 16), 240), :] = dot(gather[...], right).astype(BF)

    def normed_grad(k):
        pieces = []
        for block in (0, 1):
            for strand in (0, 1):
                first = 8 + CHIP0 + block * OWN + ((2 - k) if strand == 0 else (k - 2))
                pieces.append(gpf[strand, first : first + OWN, :])
        left = jnp.concatenate(pieces, axis=0).astype(BF)
        term = dot_nt(left, wun[k * C : (k + 1) * C, :]).reshape(2, 2, OWN, C)
        gnb[...] = term if k == 0 else gnb[...] + term

    later(16, 4, pack_group)
    for k in range(TAPS):
        todo.append(functools.partial(normed_grad, k))

    def give_normed():
        live["gn"] = put(gnb.at[other], gnx, partner)

    todo.append(give_normed)

    def serve(colour, way, dist):
        q, n, who = rings[colour]
        sign, half = ways[way]
        live[colour, sign, half].wait_recv()
        if dist > 1:
            got = ring_slot(colour, sign, half, dist)
            add = part(dwb, colour, rem(q + sign * (dist - 1) + n, n), half)
            got[...] = (got[...].astype(F32) + add[...].astype(F32)).astype(BF)
            live[colour, sign, half] = ring_give(colour, sign, half, dist - 1, got)

    def ring_total(colour, half):
        q = rings[colour][0]
        total = part(dwb, colour, q, half)[...].astype(F32)
        for sign in (1, -1):
            total = total + ring_slot(colour, sign, half, 1)[...].astype(F32)
        return total.astype(BF)

    def finish_gain():
        live["gn"].wait_recv()
        at = mine
        inverse = inv_ref[at, :]
        v, vp = xe[at, :].astype(F32), xp[at, :].astype(F32)
        gn = gnb[core, 0] + gnx[0]
        gr = gnb[core, 1] + gnx[1]
        gnb[core, 0] = gn
        gnb[core, 1] = gr
        gain_part = jnp.sum(gn * v * inverse + gr * vp * inverse, 0, keepdims=True)
        for j in range(C // 128):
            gsum[j : j + 1, :] = gain_part[:, j * 128 : (j + 1) * 128]
        live["to_z"] = [put(gsum, gz.at[o - 1], in_z(o)) for o in range(1, NZ)]

    def finish_grad():
        at = mine
        inverse = inv_ref[at, :]
        cube = inverse * inverse * inverse
        v, vp = xe[at, :].astype(F32), xp[at, :].astype(F32)
        sf, sr = gnb[core, 0] * gain2[...], gnb[core, 1] * gain2[...]
        grad_r = 0.5 * cp[at, :].astype(F32) + inverse * sr - vp * (cube * jnp.mean(sr * vp, -1, keepdims=True))
        back = dot(grad_r.astype(BF), perm[...])
        grad_f = 0.5 * ce[at, :].astype(F32) + inverse * sf - v * (cube * jnp.mean(sf * v, -1, keepdims=True))
        grad_ref[...] = (grad_f + back).astype(BF)

    def finish_out():
        f_there.wait_recv()
        r_there.wait_recv()
        low = core == 0
        mine_f, their_f = resf[mine, :], rfx[...]
        mr, tr = resr[mine, :].astype(F32), rrx[...].astype(F32)
        full_r = jnp.concatenate([jnp.where(low, mr, tr), jnp.where(low, tr, mr)], axis=1)
        back_r = dot(full_r.astype(BF), perm[...])
        full_f = jnp.concatenate(
            [jnp.where(low, mine_f, their_f), jnp.where(low, their_f, mine_f)], axis=1
        )
        out_ref[...] = (0.5 * (full_f + back_r)).astype(BF)

    todo.append(finish_out)
    todo.append(finish_gain)
    todo.append(finish_grad)

    def gathered(own, slots):
        total = own
        for one in slots:
            total = total + one
        return total

    fill(2)
    serve(2, 0, 4)
    serve(2, 1, 4)
    fill(1)
    serve(0, 0, 2)
    serve(1, 0, 2)
    fill(1)
    serve(2, 2, 3)
    serve(2, 3, 3)
    fill(1)
    serve(0, 1, 2)
    serve(1, 1, 2)
    fill(1)
    serve(2, 0, 3)
    serve(2, 1, 3)
    fill(1)
    serve(2, 2, 2)
    serve(2, 3, 2)
    fill(3)
    planes = (pl.ds(far, 4), pl.ds(near, 4))
    for colour in (0, 1):
        for way in range(4):
            serve(colour, way, 1)
    for colour in (0, 1):
        for half in (0, 1):
            red4[colour, planes[half]] = ring_total(colour, half)
    part0 = [put(red4.at[0, :, rem(y + o, NY)], slot_y.at[o - 1], in_y(o)) for o in (2, 1, 3)]
    part1 = [put(red4.at[1, :, rem(x + o, NX)], slot_x.at[o - 1], in_x(o)) for o in (2, 1, 3)]
    serve(2, 0, 2)
    serve(2, 1, 2)
    fill(2)
    serve(2, 2, 1)
    serve(2, 3, 1)
    fill(1)
    serve(2, 0, 1)
    serve(2, 1, 1)
    red8[0:2] = ring_total(2, 0)
    red8[2:4] = ring_total(2, 1)
    part2 = [put(red8.at[rem(x + o, NX)], slot_2x.at[o - 1], in_x(o)) for o in (2, 1, 3)]

    for copy in part0 + part1:
        copy.wait_recv()
    one01[:, 0] = gathered(
        red4[0, :, y].astype(F32), [slot_y[o].astype(F32) for o in range(NY - 1)]
    ).astype(BF)
    one01[:, 1] = gathered(
        red4[1, :, x].astype(F32), [slot_x[o].astype(F32) for o in range(NX - 1)]
    ).astype(BF)
    last01 = [
        put(one01.at[rem(z + o, NZ)], slot_z.at[o - 1], in_z(o)) for o in (4, 3, 5, 2, 6, 1, 7)
    ]
    fill(len(todo))

    for copy in live["to_z"]:
        copy.wait_recv()
    gp_[0] = gathered(gsum[...], [gz[o] for o in range(NZ - 1)])
    to_x = [put(gp_.at[0], gx.at[o - 1], in_x(o)) for o in range(1, NX)]

    for copy in part2:
        copy.wait_recv()
    one2[...] = gathered(
        red8[x].astype(F32), [slot_2x[o].astype(F32) for o in range(NX - 1)]
    ).astype(BF)
    last2 = [put(one2.at[rem(y + o, NY)], slot_2y.at[o - 1], in_y(o)) for o in (2, 1, 3)]

    for copy in to_x:
        copy.wait_recv()
    gp_[1] = gathered(gp_[0], [gx[o] for o in range(NX - 1)])
    to_y = [put(gp_.at[1], gy.at[o - 1], in_y(o)) for o in range(1, NY)]
    for copy in last2:
        copy.wait_recv()
    fin[:, 256:384] = gathered(
        one2[y].astype(F32), [slot_2y[o].astype(F32) for o in range(NY - 1)]
    )
    for copy in to_y:
        copy.wait_recv()
    gp_[2] = gathered(gp_[1], [gy[o] for o in range(NY - 1)])
    gain_there = put(gp_.at[2], gp_.at[3], partner)
    for copy in last01:
        copy.wait_recv()
    for j in (0, 1):
        fin[:, j * 128 : (j + 1) * 128] = gathered(
            one01[z, j].astype(F32), [slot_z[o, j].astype(F32) for o in range(NZ - 1)]
        )
    theirs16 = pl.ds(pl.multiple_of(other * 16, 16), 16)
    fin_there = put(fin.at[theirs16], finx, partner)
    gk_ref[:, half_cols] = fin[mine16, :]
    fin_there.wait_recv()
    gk_ref[:, other_cols] = finx[...]
    gain_there.wait_recv()
    total = gp_[2] + gp_[3]
    flat = iota((8, 128), 0) * 128 + iota((8, 128), 1)
    picked = jnp.zeros((8, 128), F32)
    for j in range(3):
        chosen = jnp.where(flat == (s * 8 + d) * 3 + j, total, 0.0)
        value = jnp.sum(jnp.sum(chosen, 1, keepdims=True), 0, keepdims=True)
        picked = jnp.where(iota((8, 128), 1) == j, value, picked)
    gg_ref[...] = picked

    for copy in started:
        copy.wait_send()
    for copy in edges:
        copy.wait_send()


def scratch():
    v = pltpu.VMEM
    dma = pltpu.SemaphoreType.DMA
    return [
        v((ROWS, C), BF), v((ROWS, C), BF), v((ROWS, C), BF), v((ROWS, C), BF),
        v((C, C), BF), v((ROWS, 1), F32),
        v((2, ROWS + 16, C), F32), v((2 * ROWS, TAPS * C + 128), BF),
        v((2 * ROWS, 4096), BF), v((4096, 512), BF),
        v((3, NZ, NX, NY, 32, 128), BF), v((3, NZ, NX, NY, 32, 128), BF),
        v((2 * ROWS, HALF), F32), v((ROWS, HALF), F32), v((ROWS, HALF), BF),
        v((2, ROWS + 16, HALF), F32), v((2, ROWS, HALF), BF),
        v((TAPS * C, HALF), BF),
        v((2, 2, OWN, C), F32), v((2, OWN, C), F32),
        v((OWN, HALF), F32), v((OWN, HALF), BF),
        v((2, 4, 2, 4, 4, 32, 128), BF), v((4, 4, 2, NY, 32, 128), BF),
        v((2, NZ, 4, 32, 128), BF), v((NX, NY, 32, 128), BF),
        v((3, NZ, 32, 128), BF), v((3, NZ, 32, 128), BF),
        v((3, NY, 32, 128), BF),
        v((NZ, 2, 32, 128), BF), v((NY, 32, 128), BF),
        v((7, 2, 32, 128), BF), v((3, 32, 128), BF),
        v((8, 128), F32), v((7, 8, 128), F32), v((3, 8, 128), F32), v((3, 8, 128), F32),
        v((4, 8, 128), F32),
        v((32, HALF), F32), v((16, HALF), F32),
        v((PHASES + 384, 256), BF), v((240, 256), BF),
        v((16, C), F32), v((2, 3, 16, 128), BF), v((1, C), F32),
        dma((MSGS,)), dma((MSGS,)), dma((3,)), dma((6, 2)),
    ]


def hand_over(a, b, c, d, a_out, b_out, c_out, d_out):
    a_out[0] = a[...]
    b_out[0] = b[...]
    c_out[...] = c[0:15, :]
    for j in range(3):
        d_out[j] = d[0, j]


def per_device(activations, cotangent, weights, norm_gain, pairing):
    vmem = pl.BlockSpec(memory_space=pltpu.VMEM)
    anywhere = pl.BlockSpec(memory_space=pl.ANY)
    combined, grad_input, grad_kernel, grad_gain = pl.pallas_call(
        kernel,
        out_shape=(
            jax.ShapeDtypeStruct((OWN, C), BF),
            jax.ShapeDtypeStruct((OWN, C), BF),
            jax.ShapeDtypeStruct((16, C), F32),
            jax.ShapeDtypeStruct((8, 128), F32),
        ),
        in_specs=[anywhere, anywhere, vmem, vmem, vmem],
        out_specs=(vmem, vmem, vmem, vmem),
        scratch_shapes=scratch(),
        compiler_params=pltpu.CompilerParams(
            collective_id=0, has_side_effects=True, vmem_limit_bytes=60 * 2**20
        ),
        name="strands",
    )(activations, cotangent, weights, norm_gain, pairing)
    return pl.pallas_call(
        hand_over,
        out_shape=(
            jax.ShapeDtypeStruct((1, OWN, C), BF),
            jax.ShapeDtypeStruct((1, OWN, C), BF),
            jax.ShapeDtypeStruct((15, C), F32),
            jax.ShapeDtypeStruct((3,), F32),
        ),
        in_specs=[vmem, vmem, vmem, vmem],
        out_specs=(vmem, vmem, vmem, pl.BlockSpec(memory_space=pltpu.SMEM)),
        name="results",
    )(combined, grad_input, grad_kernel, grad_gain)


def solution(mesh):
    placed = (P("dp", "seq", None), P("dp", "seq", None), P(("seq", "dp"), None), P(), P())
    return jax.shard_map(
        per_device,
        mesh=mesh,
        in_specs=placed,
        out_specs=(
            P("dp", "seq", None),
            P("dp", "seq", None),
            P(("seq", "dp"), None),
            P(("seq", "dp")),
        ),
        check_vma=False,
    )
```
